32 devices in a mesh: groups: 2 (over x), ctx: 8 (over z, y), head: 2 (over core).
Axes of the slice: x: 2, y: 2, z: 4, core: 2. Of those that a mesh axis runs over, the one named last changes fastest.
Arguments:
- queries: bfloat16 [4096, 2048], P(('groups', 'ctx'), 'head'), parts along dimension 0, may hold values from -180 to 180
- keys: bfloat16 [4096, 2048], P(('groups', 'ctx'), 'head'), parts along dimension 0, may hold values from -6 to 6
- values: bfloat16 [4096, 2048], P(('groups', 'ctx'), 'head'), parts along dimension 0, may hold values from -6 to 6
- out_weight: bfloat16 [2048, 2048], P(None, 'head'), may hold values from -0.125 to 0.125
- random_blocks: int32 [32, 3], P('groups'), parts along dimension 0, may hold values from 0 to 15, as said below
- window_blocks: int32 [32], P(('groups', 'ctx')), parts along dimension 0, may hold values from 0 to 1
- global_blocks: int32 [4], P('groups'), parts along dimension 0, may hold values from 0 to 15, as said below
Outputs:
- layer_out: bfloat16 [4096, 2048], P(('groups', 'ctx'), 'head'), parts along dimension 0
The draws below stay inside these ranges and needn't reach their ends.
There are 2 independent parts, one for each index of `groups`. The reference program is written for one: setup_inputs(seed, part) draws one part's arguments, and reference() takes and returns one part's arrays. A program takes and returns all parts, laid end to end along the dimension named above; an argument that names none is the same for every part. Nothing has to cross between parts.
Inputs may be any that keep to these rules, and one draw needn't show every extreme that they name: `random_blocks`: the random blocks named in the rows of one index j of ctx (rows j * 2 to j * 2 + 1) lie outside blocks j * 2 to j * 2 + 1; counted with repeats, at most 1 of them lie in the blocks k * 2 to k * 2 + 1 of any one other index k, and exactly 1 for some k. `global_blocks`: 2 different block numbers.
All inputs are finite; a program needn't handle non-finite values.
Results may differ from the reference program's by a relative error of at most 0.0055.
Values may be sent and summed in bfloat16 or wider, within the bound.
A program may use at most 128 MiB of HBM per device.

```python
import math
import jax
import jax.numpy as jnp
from jax import lax

HEADS = 16
HEAD = 128
D_OUT = 2048
BLOCK = 128
WMAX = 1
GLOB = 2
RAND = 3
BLK_DEV = 2
BLOCKS = 16
TOKENS = 2048


def draw_pair(key):
    width_all = HEADS * HEAD
    key_draw = jnp.clip(jax.random.normal(jax.random.fold_in(key, 11), (TOKENS, width_all), jnp.float32), -6.0, 6.0)
    query_draw = jnp.clip(jax.random.normal(jax.random.fold_in(key, 12), (TOKENS, width_all), jnp.float32), -6.0, 6.0)
    return (query_draw, key_draw)


def draw_queries(key, part):
    return draw_pair(key)[0].astype(jnp.bfloat16)


def draw_keys(key, part):
    return draw_pair(key)[1].astype(jnp.bfloat16)


def draw_random_blocks(key, part):
    dev_count = BLOCKS // BLK_DEV
    request_count = BLK_DEV * RAND
    dev_keys = jax.random.split(jax.random.fold_in(key, 7), dev_count)
    orders = jax.vmap(lambda subkey: jax.random.permutation(subkey, dev_count - 1))(dev_keys)
    cycle_pos = jnp.arange(request_count) % (dev_count - 1)
    owner_step = orders[:, cycle_pos] + 1
    shuffle_keys = jax.random.split(jax.random.fold_in(key, 8), dev_count)
    shuffles = jax.vmap(lambda subkey: jax.random.permutation(subkey, request_count))(shuffle_keys)
    owner_step = jnp.take_along_axis(owner_step, shuffles, axis=1)
    dev_index = jnp.arange(dev_count)[:, None]
    owners = (dev_index + owner_step) % dev_count
    within = jax.random.randint(jax.random.fold_in(key, 9), (dev_count, request_count), 0, BLK_DEV)
    return (owners * BLK_DEV + within).reshape(BLOCKS, RAND).astype(jnp.int32)


def draw_global_blocks(key, part):
    return jax.random.permutation(jax.random.fold_in(key, 5), BLOCKS)[:GLOB].astype(jnp.int32)


def touch_ends(array, stream_key, smallest, top_value):
    longest = array.shape.index(max(array.shape))
    spots = []
    for shift in (0, 1):
        where = [jax.random.randint(jax.random.fold_in(stream_key, axis), (), 0, length) for axis, length in enumerate(array.shape)]
        where[longest] = (where[longest] + shift) % array.shape[longest]
        spots.append(tuple(where))
    return array.at[spots[0]].set(smallest).at[spots[1]].set(top_value)


def levels(rng, dims, pieces, low, largest):
    factor_of, own = 1.0, jax.random.fold_in(rng, 6)
    for dim, shards_of in pieces:
        steps = jnp.exp(jax.random.uniform(jax.random.fold_in(own, dim), (shards_of,), jnp.float32, low / len(pieces), largest / len(pieces)))
        factor_of = factor_of * jnp.repeat(steps, dims[dim] // shards_of).reshape([-1 if axis == dim else 1 for axis in range(len(dims))])
    return factor_of


def centred(own_key, shape, deviation, most, cuts=(), held_as=jnp.bfloat16):
    entries = deviation * jax.random.normal(own_key, shape, jnp.float32)
    if cuts:
        entries = entries * levels(own_key, shape, cuts, -0.22, 0.18)
    return jnp.clip(entries, -most, most).astype(held_as)


def setup_inputs(seed: int = 0, part: int = 0) -> dict:
    arg_keys = jax.random.split(jax.random.key(seed), 8)
    part_splits = jax.random.split(jax.random.fold_in(arg_keys[7], part), 8)
    queries = draw_queries(jax.random.fold_in(jax.random.fold_in(arg_keys[7], part), 71), part)
    keys = draw_keys(jax.random.fold_in(jax.random.fold_in(arg_keys[7], part), 71), part)
    values = centred(part_splits[2], (TOKENS, HEADS * HEAD), 1.0, 6.0, ((0, 8), (1, 2)))
    out_weight = centred(arg_keys[3], (HEADS * HEAD, D_OUT), (HEADS * HEAD) ** -0.5, 0.125, ((1, 2),))
    random_blocks = draw_random_blocks(jax.random.fold_in(jax.random.fold_in(arg_keys[7], part), 71), part)
    window_blocks = touch_ends(jax.random.randint(part_splits[5], (BLOCKS,), 0, WMAX + 1), jax.random.fold_in(part_splits[5], 1), 0, WMAX).astype(jnp.int32)
    global_blocks = draw_global_blocks(jax.random.fold_in(jax.random.fold_in(arg_keys[7], part), 71), part)
    return dict(queries=queries, keys=keys, values=values, out_weight=out_weight, random_blocks=random_blocks, window_blocks=window_blocks, global_blocks=global_blocks)


LARGE_NEG = -1e+30

def split_heads(tensor):
    return tensor.reshape(tensor.shape[:-1] + (tensor.shape[-1] // HEAD, HEAD))

def block_partial(query_rows, key_rows, value_rows):
    query_heads = split_heads(query_rows).astype(jnp.float32)
    key_heads = split_heads(key_rows).astype(jnp.float32)
    value_heads = split_heads(value_rows).astype(jnp.float32)
    scores = jnp.einsum('gqhd,gckhd->gchqk', query_heads, key_heads) * (1.0 / math.sqrt(HEAD))
    row_peak = lax.optimization_barrier(jnp.max(scores, axis=-1))
    weights = jnp.exp(scores - row_peak[..., None])
    row_total = lax.optimization_barrier(jnp.sum(weights, axis=-1))
    rounded = lax.optimization_barrier(weights.astype(jnp.bfloat16)).astype(jnp.float32)
    partial_out = jnp.einsum('gchqk,gckhd->gcqhd', rounded, value_heads)
    partial_out = partial_out.reshape(partial_out.shape[:-2] + (-1,))
    return (partial_out, jnp.swapaxes(row_peak, -1, -2), jnp.swapaxes(row_total, -1, -2))

def combine(partial_out, row_peak, row_total, used_flags):
    used_mask = used_flags[:, :, None, None]
    best_peak = lax.optimization_barrier(jnp.max(jnp.where(used_mask, row_peak, LARGE_NEG), axis=1, keepdims=True))
    factor = jnp.where(used_mask, jnp.exp(row_peak - best_peak), 0.0)
    weighted = lax.optimization_barrier(jnp.sum(split_heads(partial_out) * factor[..., None], axis=1))
    normalizer = lax.optimization_barrier(jnp.sum(row_total * factor, axis=1))
    result = weighted / normalizer[..., None]
    return result.reshape(result.shape[:-2] + (-1,))

def candidates(first_block, block_count, widths, global_ids, random_rows, total_blocks):
    query_ids = first_block + jnp.arange(block_count, dtype=jnp.int32)
    offsets = jnp.arange(-WMAX, WMAX + 1, dtype=jnp.int32)
    window_ids = query_ids[:, None] + offsets[None, :]
    window_valid = (jnp.abs(offsets)[None, :] <= widths[:, None]) & (window_ids >= 0) & (window_ids < total_blocks)
    global_rows = jnp.broadcast_to(global_ids[None, :], (block_count, GLOB)).astype(jnp.int32)
    block_ids = jnp.concatenate([window_ids, global_rows, random_rows.astype(jnp.int32)], axis=1)
    valid = jnp.concatenate([window_valid, jnp.ones((block_count, GLOB + RAND), dtype=bool)], axis=1)
    width_all = block_ids.shape[1]
    same_block = block_ids[:, :, None] == block_ids[:, None, :]
    earlier = jnp.arange(width_all)[None, :] < jnp.arange(width_all)[:, None]
    shadowed = jnp.any(same_block & valid[:, None, :] & earlier[None, :, :], axis=2)
    return (block_ids, valid & jnp.logical_not(shadowed))

def reference(queries, keys, values, out_weight, random_blocks, window_blocks, global_blocks):
    tok_total, row_width = queries.shape
    total_blocks = tok_total // BLOCK
    query_blocks = queries.reshape(total_blocks, BLOCK, row_width)
    key_blocks = keys.reshape(total_blocks, BLOCK, row_width)
    value_blocks = values.reshape(total_blocks, BLOCK, row_width)
    block_ids, used_flags = candidates(0, total_blocks, window_blocks, global_blocks, random_blocks, total_blocks)
    clipped_ids = jnp.clip(block_ids, 0, total_blocks - 1).astype(jnp.int32)

    def attend(inputs):
        query_one, chosen_ids, used_row = inputs
        parts = block_partial(query_one[None], key_blocks[chosen_ids][None], value_blocks[chosen_ids][None])
        return combine(parts[0], parts[1], parts[2], used_row[None])[0].astype(jnp.bfloat16)
    attended = lax.map(attend, (query_blocks, clipped_ids, used_flags)).reshape(tok_total, row_width)
    return jnp.dot(attended, out_weight, preferred_element_type=jnp.float32).astype(jnp.bfloat16)
```

```python
import functools
import math

import jax
import jax.numpy as jnp
from jax import lax
from jax.experimental import pallas as pl
from jax.experimental.pallas import tpu as pltpu
from jax.sharding import PartitionSpec as P

HEAD = 128
BLOCK = 128
WMAX = 1
GLOB = 2
RAND = 3

LARGE_NEG = -1e30
MESH = pl.DeviceIdType.MESH

K_FWD, V_FWD, K_BWD, V_BWD = range(4)


def ring_place(index, count):
    odd = index % 2
    return (1 - odd) * (index // 2) + odd * (count - 1 - index // 2)


def ring_index(place, count):
    late = place // (count // 2)
    return (1 - late) * (2 * place) + late * (2 * (count - 1 - place) + 1)


def kernel(
    count,
    random_ref,
    window_ref,
    global_ref,
    q_hbm,
    k_hbm,
    v_hbm,
    w_hbm,
    out_ref,
    q_ref,
    w_ref,
    k_all,
    v_all,
    peak_ref,
    total_ref,
    acc_ref,
    own_ref,
    other_ref,
    sum_ref,
    load_sem,
    send_sem,
    recv_sem,
    pair_send,
    pair_recv,
):
    rows, width = q_ref.shape
    heads = width // HEAD
    dev_blocks = rows // BLOCK
    half = count // 2
    position = lax.axis_index("ctx")
    side = lax.axis_index("head")
    place = ring_place(position, count)
    right = ring_index((place + 1) % count, count)
    left = ring_index((place + count - 1) % count, count)

    load_k = pltpu.make_async_copy(k_hbm, k_all.at[0], load_sem.at[0])
    load_v = pltpu.make_async_copy(v_hbm, v_all.at[0], load_sem.at[1])
    load_q = pltpu.make_async_copy(q_hbm, q_ref, load_sem.at[2])
    load_w = pltpu.make_async_copy(w_hbm, w_ref, load_sem.at[3])
    load_k.start()
    load_v.start()
    load_q.start()

    barrier = pltpu.get_barrier_semaphore()
    pl.semaphore_signal(barrier, inc=1, device_id={"ctx": left}, device_id_type=MESH)
    pl.semaphore_signal(barrier, inc=1, device_id={"ctx": right}, device_id_type=MESH)
    pl.semaphore_signal(barrier, inc=1, device_id={"head": 1 - side}, device_id_type=MESH)
    pl.semaphore_wait(barrier, 3)

    def hop(stream, slot):
        buffer = k_all if stream in (K_FWD, K_BWD) else v_all
        forward = stream in (K_FWD, V_FWD)
        source = slot - 1 if forward else (slot + 1) % count
        return pltpu.make_async_remote_copy(
            src_ref=buffer.at[source],
            dst_ref=buffer.at[slot],
            send_sem=send_sem.at[stream, slot],
            recv_sem=recv_sem.at[stream, slot],
            device_id={"ctx": right if forward else left},
            device_id_type=MESH,
        )

    load_k.wait()
    hop(K_FWD, 1).start()
    hop(K_BWD, count - 1).start()
    load_v.wait()
    hop(V_FWD, 1).start()
    hop(V_BWD, count - 1).start()
    load_q.wait()
    load_w.start()

    peak_ref[...] = jnp.full_like(peak_ref, LARGE_NEG)
    total_ref[...] = jnp.zeros_like(total_ref)
    acc_ref[...] = jnp.zeros_like(acc_ref)
    scale = math.log2(math.e) / math.sqrt(HEAD)

    def use_bias(slot):
        owner = ring_index((place + count - slot) % count, count)
        query_rows = lax.broadcasted_iota(jnp.int32, (rows, rows), 0) // BLOCK
        key_cols = lax.broadcasted_iota(jnp.int32, (rows, rows), 1) // BLOCK
        bias = jnp.full((rows, rows), LARGE_NEG, jnp.float32)
        for a in range(dev_blocks):
            query_block = position * dev_blocks + a
            for b in range(dev_blocks):
                key_block = owner * dev_blocks + b
                offset = jnp.abs(key_block - query_block)
                used = (offset <= window_ref[a]) & (offset <= WMAX)
                for g in range(GLOB):
                    used = used | (global_ref[g] == key_block)
                for r in range(RAND):
                    used = used | (random_ref[query_block, r] == key_block)
                value = jnp.where(used, 0.0, LARGE_NEG)
                bias = jnp.where((query_rows == a) & (key_cols == b), value, bias)
        return bias

    def attend(slot):
        bias = use_bias(slot)

        def one_head(h, carry):
            cols = pl.ds(pl.multiple_of(h * HEAD, HEAD), HEAD)
            scores = lax.dot_general(
                q_ref[:, cols],
                k_all[slot, :, cols],
                (((1,), (1,)), ((), ())),
                preferred_element_type=jnp.float32,
            )
            scores = scores * scale + bias
            old_peak = peak_ref[h]
            new_peak = jnp.maximum(old_peak, jnp.max(scores, axis=1, keepdims=True))
            weights = jnp.exp2(scores - new_peak[:, :1])
            fade = jnp.exp2(old_peak - new_peak)
            part = jnp.dot(
                weights.astype(jnp.bfloat16),
                v_all[slot, :, cols],
                preferred_element_type=jnp.float32,
            )
            lanes = weights[:, :HEAD]
            for c in range(1, rows // HEAD):
                lanes = lanes + weights[:, c * HEAD : (c + 1) * HEAD]
            peak_ref[h] = new_peak
            total_ref[h] = total_ref[h] * fade + lanes
            acc_ref[h] = acc_ref[h] * fade + part
            return carry

        lax.fori_loop(0, heads, one_head, 0, unroll=2)

    def advance(step, last):
        back = count - step
        hop(K_FWD, step).wait_recv()
        hop(K_FWD, step + 1).start()
        hop(K_BWD, back).wait_recv()
        if not last:
            hop(K_BWD, back - 1).start()
        hop(V_BWD, back).wait_recv()
        hop(V_BWD, back - 1).start()
        hop(V_FWD, step).wait_recv()
        if not last:
            hop(V_FWD, step + 1).start()
        attend(step)
        attend(back)

    attend(0)

    def middle(step, carry):
        advance(step, False)
        return carry

    lax.fori_loop(1, half - 1, middle, 0)
    advance(half - 1, True)
    hop(K_FWD, half).wait_recv()
    hop(V_BWD, half).wait_recv()
    attend(half)

    for h in range(heads):
        total = jnp.sum(total_ref[h], axis=1, keepdims=True)
        own_ref[:, h * HEAD : (h + 1) * HEAD] = (acc_ref[h] / total).astype(jnp.bfloat16)

    exchange = pltpu.make_async_remote_copy(
        src_ref=own_ref,
        dst_ref=other_ref,
        send_sem=pair_send,
        recv_sem=pair_recv,
        device_id={"head": 1 - side},
        device_id_type=MESH,
    )
    exchange.start()
    load_w.wait()
    own_rows = pl.ds(pl.multiple_of(side * width, width), width)
    other_rows = pl.ds(pl.multiple_of((1 - side) * width, width), width)
    out_width = out_ref.shape[1]
    tile = min(256, out_width)

    def own_part(t, carry):
        cols = pl.ds(pl.multiple_of(t * tile, tile), tile)
        sum_ref[:, cols] = jnp.dot(
            own_ref[...], w_ref[own_rows, cols], preferred_element_type=jnp.float32
        )
        return carry

    lax.fori_loop(0, out_width // tile, own_part, 0)
    exchange.wait()

    def other_part(t, carry):
        cols = pl.ds(pl.multiple_of(t * tile, tile), tile)
        part = jnp.dot(
            other_ref[...], w_ref[other_rows, cols], preferred_element_type=jnp.float32
        )
        out_ref[:, cols] = (sum_ref[:, cols] + part).astype(out_ref.dtype)
        return carry

    lax.fori_loop(0, out_width // tile, other_part, 0)

    def drain(step, carry):
        hop(K_FWD, step).wait_send()
        hop(V_FWD, step).wait_send()
        hop(K_BWD, count - step).wait_send()
        hop(V_BWD, count - step).wait_send()
        return carry

    lax.fori_loop(1, half, drain, 0)
    hop(K_FWD, half).wait_send()
    hop(V_BWD, half).wait_send()


def per_device(queries, keys, values, out_weight, random_blocks, window_blocks, global_blocks):
    count = lax.axis_size("ctx")
    rows, width = queries.shape
    heads = width // HEAD
    out_width = out_weight.shape[1]
    smem = pl.BlockSpec(memory_space=pltpu.SMEM)
    hbm = pl.BlockSpec(memory_space=pl.ANY)
    return pl.pallas_call(
        functools.partial(kernel, count),
        out_shape=jax.ShapeDtypeStruct((rows, out_width), jnp.bfloat16),
        in_specs=[smem] * 3 + [hbm] * 4,
        out_specs=pl.BlockSpec(memory_space=pltpu.VMEM),
        scratch_shapes=[
            pltpu.VMEM((rows, width), jnp.bfloat16),
            pltpu.VMEM(out_weight.shape, jnp.bfloat16),
            pltpu.VMEM((count, rows, width), jnp.bfloat16),
            pltpu.VMEM((count, rows, width), jnp.bfloat16),
            pltpu.VMEM((heads, rows, HEAD), jnp.float32),
            pltpu.VMEM((heads, rows, HEAD), jnp.float32),
            pltpu.VMEM((heads, rows, HEAD), jnp.float32),
            pltpu.VMEM((rows, width), jnp.bfloat16),
            pltpu.VMEM((rows, width), jnp.bfloat16),
            pltpu.VMEM((rows, out_width), jnp.float32),
            pltpu.SemaphoreType.DMA((4,)),
            pltpu.SemaphoreType.DMA((4, count)),
            pltpu.SemaphoreType.DMA((4, count)),
            pltpu.SemaphoreType.DMA,
            pltpu.SemaphoreType.DMA,
        ],
        compiler_params=pltpu.CompilerParams(
            collective_id=0, has_side_effects=True, vmem_limit_bytes=60 * 1024 * 1024
        ),
    )(random_blocks, window_blocks, global_blocks, queries, keys, values, out_weight)


def solution(mesh):
    placed = (
        P(("groups", "ctx"), "head"),
        P(("groups", "ctx"), "head"),
        P(("groups", "ctx"), "head"),
        P(None, "head"),
        P("groups", None),
        P(("groups", "ctx")),
        P("groups"),
    )
    return jax.shard_map(
        per_device,
        mesh=mesh,
        in_specs=placed,
        out_specs=P(("groups", "ctx"), "head"),
        check_vma=False,
    )
```

```python
import functools
import math

import jax
import jax.numpy as jnp
from jax import lax
from jax.experimental import pallas as pl
from jax.experimental.pallas import tpu as pltpu
from jax.sharding import PartitionSpec as P

HEAD = 128
BLOCK = 128
WMAX = 1
GLOB = 2
RAND = 3

LARGE_NEG = -1e30
MESH = pl.DeviceIdType.MESH

K_FWD, V_FWD, K_BWD, V_BWD = range(4)


def ring_place(index, count):
    odd = index % 2
    return (1 - odd) * (index // 2) + odd * (count - 1 - index // 2)


def ring_index(place, count):
    late = place // (count // 2)
    return (1 - late) * (2 * place) + late * (2 * (count - 1 - place) + 1)


def kernel(
    count,
    random_ref,
    window_ref,
    global_ref,
    q_hbm,
    k_hbm,
    v_hbm,
    w_hbm,
    out_ref,
    q_ref,
    w_ref,
    k_all,
    v_all,
    peak_ref,
    total_ref,
    acc_ref,
    own_ref,
    other_ref,
    sum_ref,
    load_sem,
    send_sem,
    recv_sem,
    last_send,
    last_recv,
    pair_send,
    pair_recv,
):
    rows, width = q_ref.shape
    heads = width // HEAD
    dev_blocks = rows // BLOCK
    half = count // 2
    position = lax.axis_index("ctx")
    side = lax.axis_index("head")
    place = ring_place(position, count)
    right = ring_index((place + 1) % count, count)
    left = ring_index((place + count - 1) % count, count)

    load_k = pltpu.make_async_copy(k_hbm, k_all.at[0], load_sem.at[0])
    load_v = pltpu.make_async_copy(v_hbm, v_all.at[0], load_sem.at[1])
    load_q = pltpu.make_async_copy(q_hbm, q_ref, load_sem.at[2])
    load_w = pltpu.make_async_copy(w_hbm, w_ref, load_sem.at[3])
    load_k.start()
    load_v.start()
    load_q.start()

    barrier = pltpu.get_barrier_semaphore()
    pl.semaphore_signal(barrier, inc=1, device_id={"ctx": left}, device_id_type=MESH)
    pl.semaphore_signal(barrier, inc=1, device_id={"ctx": right}, device_id_type=MESH)
    pl.semaphore_signal(barrier, inc=1, device_id={"head": 1 - side}, device_id_type=MESH)
    pl.semaphore_wait(barrier, 3)

    def hop(stream, slot):
        buffer = k_all if stream in (K_FWD, K_BWD) else v_all
        forward = stream in (K_FWD, V_FWD)
        source = slot - 1 if forward else (slot + 1) % count
        return pltpu.make_async_remote_copy(
            src_ref=buffer.at[source],
            dst_ref=buffer.at[slot],
            send_sem=send_sem.at[stream, slot],
            recv_sem=recv_sem.at[stream, slot],
            device_id={"ctx": right if forward else left},
            device_id_type=MESH,
        )

    load_k.wait()
    hop(K_FWD, 1).start()
    hop(K_BWD, count - 1).start()
    load_v.wait()
    hop(V_FWD, 1).start()
    hop(V_BWD, count - 1).start()
    load_q.wait()
    load_w.start()

    peak_ref[...] = jnp.full_like(peak_ref, LARGE_NEG)
    total_ref[...] = jnp.zeros_like(total_ref)
    acc_ref[...] = jnp.zeros_like(acc_ref)
    scale = math.log2(math.e) / math.sqrt(HEAD)

    def use_bias(slot):
        owner = ring_index((place + count - slot) % count, count)
        row_block = lax.broadcasted_iota(jnp.int32, (rows, HEAD), 0) // BLOCK
        biases = []
        for b in range(dev_blocks):
            key_block = owner * dev_blocks + b
            bias = jnp.full((rows, HEAD), LARGE_NEG, jnp.float32)
            for a in range(dev_blocks):
                query_block = position * dev_blocks + a
                offset = jnp.abs(key_block - query_block)
                used = (offset <= window_ref[a]) & (offset <= WMAX)
                for g in range(GLOB):
                    used = used | (global_ref[g] == key_block)
                for r in range(RAND):
                    used = used | (random_ref[query_block, r] == key_block)
                bias = jnp.where(row_block == a, jnp.where(used, 0.0, LARGE_NEG), bias)
            biases.append(bias)
        return biases

    def attend_head(slot, h, biases):
        cols = pl.ds(h * HEAD, HEAD)
        if not isinstance(h, int):
            cols = pl.ds(pl.multiple_of(h * HEAD, HEAD), HEAD)
        scores = lax.dot_general(
            q_ref[:, cols],
            k_all[slot, :, cols],
            (((1,), (1,)), ((), ())),
            preferred_element_type=jnp.float32,
        )
        scores = scores * scale
        old_peak = peak_ref[h]
        best_peak = old_peak
        parts = []
        for b, bias in enumerate(biases):
            block = scores[:, b * BLOCK : (b + 1) * BLOCK]
            row_peak = jnp.max(block, axis=1, keepdims=True)
            weights = jnp.exp2(block - row_peak)
            part = jnp.dot(
                weights.astype(jnp.bfloat16),
                v_all[slot, b * BLOCK : (b + 1) * BLOCK, cols],
                preferred_element_type=jnp.float32,
            )
            used_peak = row_peak + bias
            best_peak = jnp.maximum(best_peak, used_peak)
            parts.append((used_peak, weights, part))
        fade = jnp.exp2(old_peak - best_peak)
        total = total_ref[h] * fade
        acc = acc_ref[h] * fade
        for used_peak, weights, part in parts:
            factor = jnp.exp2(used_peak - best_peak)
            total = total + weights * factor
            acc = acc + part * factor
        return best_peak, total, acc

    def attend(slot):
        biases = use_bias(slot)

        def one_head(h, carry):
            peak_ref[h], total_ref[h], acc_ref[h] = attend_head(slot, h, biases)
            return carry

        lax.fori_loop(0, heads, one_head, 0, unroll=2)

    def last_hop(stream, h):
        buffer = k_all if stream == K_FWD else v_all
        forward = h % 2 == 0
        cols = pl.ds(h * HEAD, HEAD)
        return pltpu.make_async_remote_copy(
            src_ref=buffer.at[half - 1 if forward else half + 1, :, cols],
            dst_ref=buffer.at[half, :, cols],
            send_sem=last_send.at[stream, h],
            recv_sem=last_recv.at[stream, h],
            device_id={"ctx": right if forward else left},
            device_id_type=MESH,
        )

    attend(0)

    def middle(step, carry):
        back = count - step
        hop(K_FWD, step).wait_recv()
        hop(K_FWD, step + 1).start()
        hop(K_BWD, back).wait_recv()
        hop(K_BWD, back - 1).start()
        hop(V_FWD, step).wait_recv()
        hop(V_FWD, step + 1).start()
        hop(V_BWD, back).wait_recv()
        hop(V_BWD, back - 1).start()
        attend(step)
        attend(back)
        return carry

    lax.fori_loop(1, half - 1, middle, 0)

    for side_of, key_stream in ((0, K_FWD), (1, K_BWD)):
        hop(key_stream, half + 1 if side_of else half - 1).wait_recv()
        for pair in range(min(2, heads // 2)):
            last_hop(K_FWD, 2 * pair + side_of).start()
    for side_of, value_stream in ((0, V_FWD), (1, V_BWD)):
        hop(value_stream, half + 1 if side_of else half - 1).wait_recv()
        for pair in range(heads // 2):
            last_hop(V_FWD, 2 * pair + side_of).start()
            if pair + 2 < heads // 2:
                last_hop(K_FWD, 2 * (pair + 2) + side_of).start()
    attend(half - 1)
    attend(half + 1)
    load_w.wait()
    biases = use_bias(half)
    group = 2 * HEAD

    def exchange(g):
        cols = pl.ds(g * group, group)
        return pltpu.make_async_remote_copy(
            src_ref=own_ref.at[:, cols],
            dst_ref=other_ref.at[:, cols],
            send_sem=pair_send.at[g],
            recv_sem=pair_recv.at[g],
            device_id={"head": 1 - side},
            device_id_type=MESH,
        )

    def project(source, which, g):
        w_rows = pl.ds(pl.multiple_of(which * width + g * group, group), group)
        return jnp.dot(
            source[:, g * group : (g + 1) * group],
            w_ref[w_rows, :],
            preferred_element_type=jnp.float32,
        )

    groups = width // group
    for g in range(groups):
        for h in (2 * g, 2 * g + 1):
            last_hop(K_FWD, h).wait_recv()
            last_hop(V_FWD, h).wait_recv()
            _, total, acc = attend_head(half, h, biases)
            total = jnp.sum(total, axis=1, keepdims=True)
            own_ref[:, h * HEAD : (h + 1) * HEAD] = (acc / total).astype(jnp.bfloat16)
        exchange(g).start()
        if g == 0:
            sum_ref[...] = project(own_ref, side, g)
        else:
            exchange(g - 1).wait_recv()
            sum_ref[...] += project(other_ref, 1 - side, g - 1) + project(own_ref, side, g)
    exchange(groups - 1).wait_recv()
    out_ref[...] = (sum_ref[...] + project(other_ref, 1 - side, groups - 1)).astype(out_ref.dtype)

    for g in range(groups):
        exchange(g).wait_send()
    for h in range(heads):
        last_hop(K_FWD, h).wait_send()
        last_hop(V_FWD, h).wait_send()

    def drain(step, carry):
        hop(K_FWD, step).wait_send()
        hop(V_FWD, step).wait_send()
        hop(K_BWD, count - step).wait_send()
        hop(V_BWD, count - step).wait_send()
        return carry

    lax.fori_loop(1, half, drain, 0)


def per_device(queries, keys, values, out_weight, random_blocks, window_blocks, global_blocks):
    count = lax.axis_size("ctx")
    rows, width = queries.shape
    heads = width // HEAD
    out_width = out_weight.shape[1]
    smem = pl.BlockSpec(memory_space=pltpu.SMEM)
    hbm = pl.BlockSpec(memory_space=pl.ANY)
    return pl.pallas_call(
        functools.partial(kernel, count),
        out_shape=jax.ShapeDtypeStruct((rows, out_width), jnp.bfloat16),
        in_specs=[smem] * 3 + [hbm] * 4,
        out_specs=pl.BlockSpec(memory_space=pltpu.VMEM),
        scratch_shapes=[
            pltpu.VMEM((rows, width), jnp.bfloat16),
            pltpu.VMEM(out_weight.shape, jnp.bfloat16),
            pltpu.VMEM((count, rows, width), jnp.bfloat16),
            pltpu.VMEM((count, rows, width), jnp.bfloat16),
            pltpu.VMEM((heads, rows, HEAD), jnp.float32),
            pltpu.VMEM((heads, rows, HEAD), jnp.float32),
            pltpu.VMEM((heads, rows, HEAD), jnp.float32),
            pltpu.VMEM((rows, width), jnp.bfloat16),
            pltpu.VMEM((rows, width), jnp.bfloat16),
            pltpu.VMEM((rows, out_width), jnp.float32),
            pltpu.SemaphoreType.DMA((4,)),
            pltpu.SemaphoreType.DMA((4, count)),
            pltpu.SemaphoreType.DMA((4, count)),
            pltpu.SemaphoreType.DMA((2, heads)),
            pltpu.SemaphoreType.DMA((2, heads)),
            pltpu.SemaphoreType.DMA((heads // 2,)),
            pltpu.SemaphoreType.DMA((heads // 2,)),
        ],
        compiler_params=pltpu.CompilerParams(
            collective_id=0, has_side_effects=True, vmem_limit_bytes=60 * 1024 * 1024
        ),
    )(random_blocks, window_blocks, global_blocks, queries, keys, values, out_weight)


def solution(mesh):
    placed = (
        P(("groups", "ctx"), "head"),
        P(("groups", "ctx"), "head"),
        P(("groups", "ctx"), "head"),
        P(None, "head"),
        P("groups", None),
        P(("groups", "ctx")),
        P("groups"),
    )
    return jax.shard_map(
        per_device,
        mesh=mesh,
        in_specs=placed,
        out_specs=P(("groups", "ctx"), "head"),
        check_vma=False,
    )
```

```python
import functools
import math

import jax
import jax.numpy as jnp
from jax import lax
from jax.experimental import pallas as pl
from jax.experimental.pallas import tpu as pltpu
from jax.sharding import PartitionSpec as P

HEAD = 128
BLOCK = 128
WMAX = 1
GLOB = 2
RAND = 3

LARGE_NEG = -1e30
MESH = pl.DeviceIdType.MESH

K_FWD, V_FWD, K_BWD, V_BWD = range(4)


def ring_place(index, count):
    odd = index % 2
    return (1 - odd) * (index // 2) + odd * (count - 1 - index // 2)


def ring_index(place, count):
    late = place // (count // 2)
    return (1 - late) * (2 * place) + late * (2 * (count - 1 - place) + 1)


def kernel(
    count,
    random_ref,
    window_ref,
    global_ref,
    q_hbm,
    k_hbm,
    v_hbm,
    w_hbm,
    out_any,
    q_ref,
    w_ref,
    k_all,
    v_all,
    peak_ref,
    total_ref,
    acc_ref,
    own_ref,
    other_ref,
    sum_ref,
    out_ref,
    load_sem,
    send_sem,
    recv_sem,
    last_send,
    last_recv,
    pair_send,
    pair_recv,
):
    rows, width = q_ref.shape
    heads = width // HEAD
    dev_blocks = rows // BLOCK
    half = count // 2
    position = lax.axis_index("ctx")
    side = lax.axis_index("head")
    place = ring_place(position, count)
    right = ring_index((place + 1) % count, count)
    left = ring_index((place + count - 1) % count, count)

    load_k = pltpu.make_async_copy(k_hbm, k_all.at[0], load_sem.at[0])
    load_v = pltpu.make_async_copy(v_hbm, v_all.at[0], load_sem.at[1])
    load_q = pltpu.make_async_copy(q_hbm, q_ref, load_sem.at[2])
    load_w = pltpu.make_async_copy(w_hbm, w_ref, load_sem.at[3])
    load_k.start()
    load_v.start()
    load_q.start()

    barrier = pltpu.get_barrier_semaphore()
    pl.semaphore_signal(barrier, inc=1, device_id={"ctx": left}, device_id_type=MESH)
    pl.semaphore_signal(barrier, inc=1, device_id={"ctx": right}, device_id_type=MESH)
    pl.semaphore_signal(barrier, inc=1, device_id={"head": 1 - side}, device_id_type=MESH)
    pl.semaphore_wait(barrier, 3)

    def hop(stream, slot):
        buffer = k_all if stream in (K_FWD, K_BWD) else v_all
        forward = stream in (K_FWD, V_FWD)
        source = slot - 1 if forward else (slot + 1) % count
        return pltpu.make_async_remote_copy(
            src_ref=buffer.at[source],
            dst_ref=buffer.at[slot],
            send_sem=send_sem.at[stream, slot],
            recv_sem=recv_sem.at[stream, slot],
            device_id={"ctx": right if forward else left},
            device_id_type=MESH,
        )

    load_k.wait()
    hop(K_FWD, 1).start()
    hop(K_BWD, count - 1).start()
    load_v.wait()
    hop(V_FWD, 1).start()
    hop(V_BWD, count - 1).start()
    load_q.wait()
    load_w.start()

    peak_ref[...] = jnp.full_like(peak_ref, LARGE_NEG)
    total_ref[...] = jnp.zeros_like(total_ref)
    acc_ref[...] = jnp.zeros_like(acc_ref)
    scale = math.log2(math.e) / math.sqrt(HEAD)

    def use_bias(slot):
        owner = ring_index((place + count - slot) % count, count)
        row_block = lax.broadcasted_iota(jnp.int32, (rows, HEAD), 0) // BLOCK
        biases = []
        for b in range(dev_blocks):
            key_block = owner * dev_blocks + b
            bias = jnp.full((rows, HEAD), LARGE_NEG, jnp.float32)
            for a in range(dev_blocks):
                query_block = position * dev_blocks + a
                offset = jnp.abs(key_block - query_block)
                used = (offset <= window_ref[a]) & (offset <= WMAX)
                for g in range(GLOB):
                    used = used | (global_ref[g] == key_block)
                for r in range(RAND):
                    used = used | (random_ref[r, query_block] == key_block)
                bias = jnp.where(row_block == a, jnp.where(used, 0.0, LARGE_NEG), bias)
            biases.append(bias)
        return biases

    def attend_head(slot, h, biases):
        cols = pl.ds(h * HEAD, HEAD)
        if not isinstance(h, int):
            cols = pl.ds(pl.multiple_of(h * HEAD, HEAD), HEAD)
        scores = lax.dot_general(
            q_ref[:, cols],
            k_all[slot, :, cols],
            (((1,), (1,)), ((), ())),
            preferred_element_type=jnp.float32,
        )
        scores = scores * scale
        old_peak = peak_ref[h]
        best_peak = old_peak
        parts = []
        for b, bias in enumerate(biases):
            block = scores[:, b * BLOCK : (b + 1) * BLOCK]
            row_peak = jnp.max(block, axis=1, keepdims=True)
            weights = jnp.exp2(block - row_peak)
            part = jnp.dot(
                weights.astype(jnp.bfloat16),
                v_all[slot, b * BLOCK : (b + 1) * BLOCK, cols],
                preferred_element_type=jnp.float32,
            )
            used_peak = row_peak + bias
            best_peak = jnp.maximum(best_peak, used_peak)
            parts.append((used_peak, weights, part))
        fade = jnp.exp2(old_peak - best_peak)
        total = total_ref[h] * fade
        acc = acc_ref[h] * fade
        for used_peak, weights, part in parts:
            factor = jnp.exp2(used_peak - best_peak)
            total = total + weights * factor
            acc = acc + part * factor
        return best_peak, total, acc

    def attend(slot):
        biases = use_bias(slot)

        def one_head(h, carry):
            peak_ref[h], total_ref[h], acc_ref[h] = attend_head(slot, h, biases)
            return carry

        lax.fori_loop(0, heads, one_head, 0, unroll=2)

    def last_hop(stream, h):
        buffer = k_all if stream == K_FWD else v_all
        forward = h % 2 == 0
        cols = pl.ds(h * HEAD, HEAD)
        return pltpu.make_async_remote_copy(
            src_ref=buffer.at[half - 1 if forward else half + 1, :, cols],
            dst_ref=buffer.at[half, :, cols],
            send_sem=last_send.at[stream, h],
            recv_sem=last_recv.at[stream, h],
            device_id={"ctx": right if forward else left},
            device_id_type=MESH,
        )

    attend(0)

    def middle(step, carry):
        back = count - step
        hop(K_FWD, step).wait_recv()
        hop(K_FWD, step + 1).start()
        hop(K_BWD, back).wait_recv()
        hop(K_BWD, back - 1).start()
        hop(V_FWD, step).wait_recv()
        hop(V_FWD, step + 1).start()
        hop(V_BWD, back).wait_recv()
        hop(V_BWD, back - 1).start()
        attend(step)
        attend(back)
        return carry

    lax.fori_loop(1, half - 1, middle, 0)

    for side_of, key_stream in ((0, K_FWD), (1, K_BWD)):
        hop(key_stream, half + 1 if side_of else half - 1).wait_recv()
        for pair in range(min(2, heads // 2)):
            last_hop(K_FWD, 2 * pair + side_of).start()
    for side_of, value_stream in ((0, V_FWD), (1, V_BWD)):
        hop(value_stream, half + 1 if side_of else half - 1).wait_recv()
        for pair in range(heads // 2):
            last_hop(V_FWD, 2 * pair + side_of).start()
            if pair + 2 < heads // 2:
                last_hop(K_FWD, 2 * (pair + 2) + side_of).start()
    attend(half - 1)
    attend(half + 1)
    load_w.wait()
    biases = use_bias(half)
    group = 2 * HEAD

    def exchange(g):
        cols = pl.ds(g * group, group)
        return pltpu.make_async_remote_copy(
            src_ref=own_ref.at[:, cols],
            dst_ref=other_ref.at[:, cols],
            send_sem=pair_send.at[g],
            recv_sem=pair_recv.at[g],
            device_id={"head": 1 - side},
            device_id_type=MESH,
        )

    def project(source, which, g):
        w_rows = pl.ds(pl.multiple_of(which * width + g * group, group), group)
        return jnp.dot(
            source[:, g * group : (g + 1) * group],
            w_ref[w_rows, :],
            preferred_element_type=jnp.float32,
        )

    groups = width // group
    for g in range(groups):
        for h in (2 * g, 2 * g + 1):
            last_hop(K_FWD, h).wait_recv()
            last_hop(V_FWD, h).wait_recv()
            _, total, acc = attend_head(half, h, biases)
            total = jnp.sum(total, axis=1, keepdims=True)
            own_ref[:, h * HEAD : (h + 1) * HEAD] = (acc / total).astype(jnp.bfloat16)
        exchange(g).start()
        if g == 0:
            sum_ref[...] = project(own_ref, side, g)
        else:
            exchange(g - 1).wait_recv()
            sum_ref[...] += project(other_ref, 1 - side, g - 1) + project(own_ref, side, g)
    exchange(groups - 1).wait_recv()
    out_ref[...] = (sum_ref[...] + project(other_ref, 1 - side, groups - 1)).astype(out_ref.dtype)

    store = pltpu.make_async_copy(out_ref, out_any, load_sem.at[4])
    store.start()
    for g in range(groups):
        exchange(g).wait_send()
    for h in range(heads):
        last_hop(K_FWD, h).wait_send()
        last_hop(V_FWD, h).wait_send()

    def drain(step, carry):
        hop(K_FWD, step).wait_send()
        hop(V_FWD, step).wait_send()
        hop(K_BWD, count - step).wait_send()
        hop(V_BWD, count - step).wait_send()
        return carry

    lax.fori_loop(1, half, drain, 0)
    store.wait()


def per_device(queries, keys, values, out_weight, random_blocks, window_blocks, global_blocks):
    count = lax.axis_size("ctx")
    rows, width = queries.shape
    heads = width // HEAD
    out_width = out_weight.shape[1]
    smem = pl.BlockSpec(memory_space=pltpu.SMEM)
    hbm = pl.BlockSpec(memory_space=pltpu.HBM)
    return pl.pallas_call(
        functools.partial(kernel, count),
        out_shape=jax.ShapeDtypeStruct((rows, out_width), jnp.bfloat16),
        in_specs=[smem] * 3 + [hbm] * 4,
        out_specs=pl.BlockSpec(memory_space=pl.ANY),
        scratch_shapes=[
            pltpu.VMEM((rows, width), jnp.bfloat16),
            pltpu.VMEM(out_weight.shape, jnp.bfloat16),
            pltpu.VMEM((count, rows, width), jnp.bfloat16),
            pltpu.VMEM((count, rows, width), jnp.bfloat16),
            pltpu.VMEM((heads, rows, HEAD), jnp.float32),
            pltpu.VMEM((heads, rows, HEAD), jnp.float32),
            pltpu.VMEM((heads, rows, HEAD), jnp.float32),
            pltpu.VMEM((rows, width), jnp.bfloat16),
            pltpu.VMEM((rows, width), jnp.bfloat16),
            pltpu.VMEM((rows, out_width), jnp.float32),
            pltpu.VMEM((rows, out_width), jnp.bfloat16),
            pltpu.SemaphoreType.DMA((5,)),
            pltpu.SemaphoreType.DMA((4, count)),
            pltpu.SemaphoreType.DMA((4, count)),
            pltpu.SemaphoreType.DMA((2, heads)),
            pltpu.SemaphoreType.DMA((2, heads)),
            pltpu.SemaphoreType.DMA((heads // 2,)),
            pltpu.SemaphoreType.DMA((heads // 2,)),
        ],
        compiler_params=pltpu.CompilerParams(
            collective_id=0, has_side_effects=True, vmem_limit_bytes=60 << 20
        ),
    )(random_blocks.T, window_blocks, global_blocks, queries, keys, values, out_weight)


def solution(mesh):
    placed = (
        P(("groups", "ctx"), "head"),
        P(("groups", "ctx"), "head"),
        P(("groups", "ctx"), "head"),
        P(None, "head"),
        P("groups", None),
        P(("groups", "ctx")),
        P("groups"),
    )
    return jax.shard_map(
        per_device,
        mesh=mesh,
        in_specs=placed,
        out_specs=P(("groups", "ctx"), "head"),
        check_vma=False,
    )
```
